512 devices in a mesh: vec: 16 (over y, x_hi), amp: 32 (over x_lo, z, core).
Axes of the slice: x: 4 (x_hi: 2, x_lo: 2; x = x_hi * 2 + x_lo), y: 8, z: 8, core: 2. Of those that a mesh axis runs over, the one named last changes fastest.
Arguments:
- chol: bfloat16 [64, 1024, 8192], P(None, 'amp', 'vec'), may hold values from -2.5 to 2.5
- amplitudes: bfloat16 [64, 256, 1024], P(None, 'amp'), may hold values from -0.125 to 0.125
- task_list: int32 [64, 4], replicated, may hold values from 0 to 63
- counts: int32 [32], replicated, may hold values from 0 to 2, as said below
Outputs:
- residual: bfloat16 [64, 256, 1024], P('vec', 'amp')
The draws below stay inside these ranges and needn't reach their ends.
Inputs may be any that keep to these rules, and one draw needn't show every extreme that they name: The counts sum to 32, and one of them equals 2.
All inputs are finite; a program needn't handle non-finite values.
Results may differ from the reference program's by a relative error of at most 0.0055.
Values may be sent and summed in bfloat16 or wider, within the bound.
A program may use at most 128 MiB of HBM per device.

```python
from functools import partial
import jax
import jax.numpy as jnp
from jax import lax

VB = 32
NAUX = 8192
OPAIRS = 256
PAIRS = 1024
GROUPS = 16
GROUP_WIDTH = 512
TILES = 64
MOST = 2
TASKS = 32
LISTS = 64
N_AMP = 32


def draw_counts(key, part):
    slot_total = N_AMP * MOST
    shuffled = jax.random.permutation(key, slot_total).astype(jnp.int32)
    busiest = shuffled[0] // MOST
    position = jnp.zeros((slot_total,), jnp.int32).at[shuffled].set(jnp.arange(slot_total, dtype=jnp.int32))
    slot_ids = jnp.arange(slot_total, dtype=jnp.int32)
    ranking = jnp.where(slot_ids // MOST == busiest, position - slot_total, position)
    chosen = jnp.argsort(ranking)[:TASKS]
    owner_ids = (chosen // MOST).astype(jnp.int32)
    return jnp.sum((owner_ids[:, None] == jnp.arange(N_AMP, dtype=jnp.int32)[None, :]).astype(jnp.int32), axis=0)


def set_ends(drawn, stream_key, low, high):
    longest = drawn.shape.index(max(drawn.shape))
    spots = []
    for shift in (0, 1):
        where = [jax.random.randint(jax.random.fold_in(stream_key, axis), (), 0, length) for axis, length in enumerate(drawn.shape)]
        where[longest] = (where[longest] + shift) % drawn.shape[longest]
        spots.append(tuple(where))
    return drawn.at[spots[0]].set(low).at[spots[1]].set(high)


def with_spikes(values, own_key, source, target, parts, factor):
    def block_of(dim):
        return (jnp.arange(values.shape[dim]) // (values.shape[dim] // parts)).reshape((-1,) + (1,) * (values.ndim - 1 - dim))

    first = jax.random.permutation(own_key, parts)[block_of(target)]
    second = (block_of(target) + parts // 2) % parts
    return jnp.where((block_of(source) == first) | (block_of(source) == second), factor * values, values)


def levels(rng, extent, split, low, high):
    def one(dim, blocks):
        steps = jax.random.uniform(jax.random.fold_in(jax.random.fold_in(rng, 6), dim), (blocks,), jnp.float32, low / len(split), high / len(split))
        return jnp.repeat(jnp.exp(steps), extent[dim] // blocks).reshape((-1,) + (1,) * (len(extent) - dim - 1))

    level = one(*split[0])
    for cut in split[1:]:
        level = level * one(*cut)
    return level


def gaussian(own_key, extent, deviation, most, cuts=(), held_as=jnp.bfloat16):
    array = jax.random.normal(own_key, extent, jnp.float32) * deviation
    if len(cuts) > 0:
        array = levels(own_key, extent, cuts, -0.22, 0.18) * array
    return jnp.clip(array, min=-most, max=most).astype(held_as)


def gaussian_with(key, dims, scale, limit, cuts, heavy, kind=jnp.bfloat16):
    array = scale * jax.random.normal(key, dims, jnp.float32)
    if cuts:
        array = array * levels(key, dims, cuts, -0.22, 0.18)
    return jnp.clip(with_spikes(array, jax.random.fold_in(key, 3), *heavy), -limit, limit).astype(kind)


def setup_inputs(seed: int = 0) -> dict:
    key_of = jax.random.split(jax.random.key(seed), 5)
    chol = gaussian_with(key_of[0], (TILES, PAIRS, NAUX), 0.125, 2.5, ((1, 32), (2, 16)), (2, 0, 16, 2.0))
    amplitudes = gaussian(key_of[1], (TILES, OPAIRS, PAIRS), (PAIRS * NAUX // 4096) ** -0.5, 0.125, ((1, 32),))
    task_list = set_ends(jax.random.randint(key_of[2], (LISTS, 4), 0, TILES), jax.random.fold_in(key_of[2], 1), 0, TILES - 1).astype(jnp.int32)
    counts = draw_counts(jax.random.fold_in(key_of[4], 71), 0)
    return dict(chol=chol, amplitudes=amplitudes, task_list=task_list, counts=counts)


def integral_tile(x_rows, y_rows):
    products = jnp.dot(x_rows, y_rows.T, preferred_element_type=jnp.float32)
    return products.reshape(VB, VB, VB, VB).transpose(0, 2, 1, 3).reshape(PAIRS, PAIRS).astype(jnp.bfloat16)


def task_term(chol, amplitudes, task_entry):
    x_groups = chol[task_entry[0]].reshape(PAIRS, GROUPS, GROUP_WIDTH).transpose(1, 0, 2)
    y_groups = chol[task_entry[1]].reshape(PAIRS, GROUPS, GROUP_WIDTH).transpose(1, 0, 2)
    amp_rows = amplitudes[task_entry[2]]

    def add_group(running, group_pair):
        integral = integral_tile(group_pair[0], group_pair[1])
        partial_term = jnp.dot(amp_rows, integral.T, preferred_element_type=jnp.float32).astype(jnp.bfloat16)
        return running + partial_term.astype(jnp.float32), None

    running, _ = lax.scan(add_group, jnp.zeros((OPAIRS, PAIRS), jnp.float32), (x_groups, y_groups))
    return running


def reference(chol, amplitudes, task_list, counts):
    offsets = jnp.cumsum(counts) - counts
    task_rank = jnp.arange(TASKS, dtype=jnp.int32)[:, None]
    inside = (task_rank >= offsets[None, :]) & (task_rank < (offsets + counts)[None, :])
    owners = jnp.arange(N_AMP, dtype=jnp.int32)[None, :]
    entries = jnp.sum(jnp.where(inside, owners * MOST + task_rank - offsets[None, :], 0), axis=1).astype(jnp.int32)
    chosen = task_list[entries]
    contribs = lax.map(partial(task_term, chol, amplitudes), chosen)
    residual = jnp.zeros((TILES, OPAIRS, PAIRS), jnp.float32).at[chosen[:, 3]].add(contribs)
    return residual.astype(jnp.bfloat16)
```

```python
import jax
import jax.numpy as jnp
from jax import lax
from jax.experimental import pallas as pl
from jax.experimental.pallas import tpu as pltpu
from jax.sharding import PartitionSpec as P

VB = 32
PAIRS = 1024
MOST = 2
TASKS = 32
N_AMP = 32
N_VEC = 16
MESH = pl.DeviceIdType.MESH
F32 = jnp.float32
BF16 = jnp.bfloat16
NT = (((1,), (1,)), ((), ()))


def compact_kernel(list_ref, counts_ref, out_ref):
    def entry(e, position):
        for k in range(4):
            out_ref[position * 4 + k] = list_ref[e, k]
        return position + jnp.where(lax.rem(e, MOST) < counts_ref[e // MOST], 1, 0)

    lax.fori_loop(0, N_AMP * MOST, entry, 0)


def compact(task_list, counts):
    return pl.pallas_call(
        compact_kernel,
        out_shape=jax.ShapeDtypeStruct(((TASKS + 1) * 4,), jnp.int32),
        in_specs=[pl.BlockSpec(memory_space=pltpu.SMEM)] * 2,
        out_specs=pl.BlockSpec(memory_space=pltpu.SMEM),
    )(task_list, counts)


def shift_of(q):
    return ((q + 1) // 2) * (2 * (q % 2) - 1)


def arrived(block, sem):
    pltpu.make_async_copy(block, block, sem).wait()


def ladder_kernel(
    task_ref, chol_hbm, amp_hbm, out_ref,
    chol_v, amp_v, xs, ys, ts, xr, yr, tr, xp, tfull, qs, vs, vr, ssum, keys, s2s, s2r, s3s, s3r,
    in_sem, x_send, x_recv, y_send, y_recv, t_send, t_recv, tv_send, tv_recv,
    v_send, v_recv, s2_send, s2_recv, s3_send, s3_recv,
):
    v = lax.axis_index("vec")
    m = lax.axis_index("amp")
    y, x_hi = v // 2, v % 2
    x_lo, z, core = m // 16, (m // 2) % 8, m % 2

    def amp_peer(j):
        return ((x_lo + (j // 2) % 2) % 2) * 16 + ((z + shift_of(j // 4) + 8) % 8) * 2 + (core + j) % 2

    def vec_peer(j):
        return (v + j) % N_VEC

    def to_amp(src, dst, send, recv, peer):
        pltpu.make_async_remote_copy(
            src_ref=src, dst_ref=dst, send_sem=send, recv_sem=recv,
            device_id={"amp": peer}, device_id_type=MESH,
        ).start()

    def to_vec(src, dst, send, recv, peer):
        pltpu.make_async_remote_copy(
            src_ref=src, dst_ref=dst, send_sem=send, recv_sem=recv,
            device_id={"vec": peer}, device_id_type=MESH,
        ).start()

    load_amp = pltpu.make_async_copy(amp_hbm, amp_v, in_sem.at[0])
    load_chol = pltpu.make_async_copy(chol_hbm, chol_v, in_sem.at[1])
    load_amp.start()
    load_chol.start()

    barrier = pltpu.get_barrier_semaphore()

    @pl.loop(1, N_AMP)
    def _(j):
        pl.semaphore_signal(barrier, inc=1, device_id={"amp": amp_peer(j)}, device_id_type=MESH)

    @pl.loop(1, N_VEC)
    def _(j):
        pl.semaphore_signal(barrier, inc=1, device_id={"vec": vec_peer(j)}, device_id_type=MESH)

    load_amp.wait()
    columns = pl.ds(pl.multiple_of(y * 128, 128), 128)

    @pl.loop(0, TASKS)
    def _(t):
        ts[t] = amp_v[task_ref[t * 4 + 2], :, columns]

    load_chol.wait()

    @pl.loop(0, TASKS)
    def _(t):
        xs[t] = chol_v[task_ref[t * 4]]
        ys[t] = chol_v[task_ref[t * 4 + 1]]

    pl.semaphore_wait(barrier, N_AMP + N_VEC - 2)

    @pl.when(core == x_hi)
    def _():
        pltpu.make_async_copy(ts.at[m], tr.at[v, m // 2], t_recv).start()

        @pl.loop(1, N_AMP)
        def _(j):
            peer = amp_peer(j)
            to_amp(ts.at[peer], tr.at[v, m // 2], t_send, t_recv, peer)

    pltpu.make_async_copy(xs.at[m], xr.at[m], x_recv).start()

    @pl.loop(1, N_AMP)
    def _(j):
        peer = amp_peer(j)
        to_amp(xs.at[peer], xr.at[m], x_send, x_recv, peer)

    pltpu.make_async_copy(ys.at[m], yr.at[x_lo, z, core], y_recv.at[0]).start()

    @pl.loop(1, N_AMP)
    def _(j):
        peer = amp_peer(j)
        to_amp(ys.at[peer], yr.at[x_lo, z, core], y_send, y_recv.at[j // 4], peer)

    arrived(tr.at[v], t_recv)

    @pl.loop(1, N_VEC)
    def _(j):
        to_vec(tr.at[v], tr.at[v], tv_send, tv_recv, vec_peer(j))

    lane = lax.broadcasted_iota(jnp.int32, (8, 256), 1)

    def place(t, held):
        return jnp.where(lane // 8 == t, task_ref[t * 4 + 3] * 8 + lane % 8, held)

    wanted = lax.fori_loop(0, TASKS, place, jnp.zeros((8, 256), jnp.int32))[:1]

    @pl.loop(0, 4)
    def _(k):
        rows = lax.broadcasted_iota(jnp.int32, (128, 256), 0) + k * 128
        keys[pl.ds(pl.multiple_of(k * 128, 128), 128), :] = jnp.where(rows == wanted, 1.0, 0.0).astype(BF16)

    arrived(xr, x_recv)

    @pl.loop(0, 8)
    def _(k):
        rows = lax.broadcasted_iota(jnp.int32, (128, 1024), 0) + k * 128
        cols = lax.broadcasted_iota(jnp.int32, (128, 1024), 1)
        pick = jnp.where(cols == (rows % 32) * 32 + rows // 32, 1.0, 0.0).astype(BF16)
        xp[pl.ds(pl.multiple_of(k * 128, 128), 128), :] = jnp.dot(
            pick, xr[...].reshape(PAIRS, 512), preferred_element_type=F32
        ).astype(BF16)

    arrived(tr.at[pl.ds(0, N_VEC - 1)], tv_recv)

    @pl.loop(0, 16)
    def _(k):
        for c in range(8):
            both = [
                jnp.concatenate([tr[2 * c, k].astype(F32), tr[2 * c + 1, k].astype(F32)], axis=0)
            ]
            tfull[pl.ds(pl.multiple_of(k * 16, 16), 16), c * 128 : c * 128 + 128] = both[0].astype(BF16)

    lanes = lax.broadcasted_iota(jnp.int32, (32, 128), 1)
    low_half = lanes < 64
    even = (lanes // 32) % 2 == 0

    @pl.loop(0, 8)
    def _(q):
        from_z = (z - shift_of(q) + 8) % 8
        arrived(yr.at[0, pl.ds(0, 2)], y_recv.at[q])
        y_rows = jnp.concatenate(
            [yr[0, from_z].reshape(64, 512), yr[1, from_z].reshape(64, 512)], axis=0
        )
        for k in range(8):
            block = lax.dot_general(
                xp[k * 128 : k * 128 + 128, :], y_rows, NT, preferred_element_type=F32
            )
            p0, p1, p2, p3 = (block[c * 32 : c * 32 + 32] for c in range(4))
            a0 = jnp.where(low_half, p0, pltpu.roll(p2, 64, 1))
            a2 = jnp.where(low_half, pltpu.roll(p0, 64, 1), p2)
            a1 = jnp.where(low_half, p1, pltpu.roll(p3, 64, 1))
            a3 = jnp.where(low_half, pltpu.roll(p1, 64, 1), p3)
            w = (
                jnp.where(even, a0, pltpu.roll(a1, 32, 1)),
                jnp.where(even, pltpu.roll(a0, 96, 1), a1),
                jnp.where(even, a2, pltpu.roll(a3, 32, 1)),
                jnp.where(even, pltpu.roll(a2, 96, 1), a3),
            )
            for b in range(4):
                qs[b * 32 : b * 32 + 32, k * 128 : k * 128 + 128] = w[b].astype(BF16)
        term = lax.dot_general(qs[...], tfull[...], NT, preferred_element_type=F32)
        for k in range(N_VEC):
            vs[q, k] = term[k * 8 : k * 8 + 8].astype(BF16)

        pltpu.make_async_copy(vs.at[q, v], vr.at[q, v], v_recv.at[q]).start()

        @pl.loop(1, N_VEC)
        def _(j):
            peer = vec_peer(j)
            to_vec(vs.at[q, peer], vr.at[q, v], v_send.at[q], v_recv.at[q], peer)

    @pl.loop(0, 8)
    def _(q):
        from_z = (z - shift_of(q) + 8) % 8
        arrived(vr.at[q], v_recv.at[q])
        total = vr[q, 0].astype(F32)
        for k in range(1, N_VEC):
            total += vr[q, k].astype(F32)
        high = total.astype(BF16).astype(F32)
        ssum[pl.ds(pl.multiple_of(from_z * 8, 8), 8), :] = high
        ssum[pl.ds(pl.multiple_of(from_z * 8 + 64, 8), 8), :] = total - high

    turned = ssum[...].T
    for k in range(N_AMP):
        s2s[k] = turned[k * 8 : k * 8 + 8].astype(BF16)

    pltpu.make_async_copy(s2s.at[m], s2r.at[m], s2_recv).start()

    @pl.loop(1, N_AMP)
    def _(j):
        peer = amp_peer(j)
        to_amp(s2s.at[peer], s2r.at[m], s2_send, s2_recv, peer)

    arrived(s2r, s2_recv)
    parts = s2r[...].astype(F32).reshape(256, 128).astype(BF16)
    tiles = jnp.dot(keys[...], parts, preferred_element_type=F32)
    tiles = tiles + pltpu.roll(tiles, 64, 1)
    low16 = lax.broadcasted_iota(jnp.int32, (16, 128), 1) < 64
    for k in range(N_VEC):
        s3s[k] = jnp.where(
            low16, tiles[k * 32 : k * 32 + 16], tiles[k * 32 + 16 : k * 32 + 32]
        ).astype(BF16)

    pltpu.make_async_copy(s3s.at[v], s3r.at[v], s3_recv).start()

    @pl.loop(1, N_VEC)
    def _(j):
        peer = vec_peer(j)
        to_vec(s3s.at[peer], s3r.at[v], s3_send, s3_recv, peer)

    arrived(s3r, s3_recv)
    out_ref[...] = s3r[...]

    @pl.when(core == x_hi)
    def _():
        arrived(ts.at[pl.ds(0, N_AMP - 1)], t_send)

    arrived(xs.at[pl.ds(0, N_AMP - 1)], x_send)
    arrived(ys.at[pl.ds(0, N_AMP - 1)], y_send)
    arrived(tr.at[pl.ds(0, N_VEC - 1)], tv_send)

    @pl.loop(0, 8)
    def _(q):
        arrived(vs.at[q, pl.ds(0, N_VEC - 1)], v_send.at[q])

    arrived(s2s.at[pl.ds(0, N_AMP - 1)], s2_send)
    arrived(s3s.at[pl.ds(0, N_VEC - 1)], s3_send)


def ladder(tasks, chol, amplitudes):
    dma = pltpu.SemaphoreType.DMA
    return pl.pallas_call(
        ladder_kernel,
        out_shape=jax.ShapeDtypeStruct((N_VEC, 16, 128), BF16),
        in_specs=[
            pl.BlockSpec(memory_space=pltpu.SMEM),
            pl.BlockSpec(memory_space=pl.ANY),
            pl.BlockSpec(memory_space=pl.ANY),
        ],
        out_specs=pl.BlockSpec(memory_space=pltpu.VMEM),
        scratch_shapes=[
            pltpu.VMEM((64, 32, 512), BF16),
            pltpu.VMEM((64, 8, 1024), BF16),
            pltpu.VMEM((32, 32, 512), BF16),
            pltpu.VMEM((32, 32, 512), BF16),
            pltpu.VMEM((32, 8, 128), BF16),
            pltpu.VMEM((32, 32, 512), BF16),
            pltpu.VMEM((2, 8, 2, 32, 512), BF16),
            pltpu.VMEM((16, 16, 8, 128), BF16),
            pltpu.VMEM((1024, 512), BF16),
            pltpu.VMEM((256, 1024), BF16),
            pltpu.VMEM((128, 1024), BF16),
            pltpu.VMEM((8, 16, 8, 256), BF16),
            pltpu.VMEM((8, 16, 8, 256), BF16),
            pltpu.VMEM((128, 256), F32),
            pltpu.VMEM((512, 256), BF16),
            pltpu.VMEM((32, 8, 128), BF16),
            pltpu.VMEM((32, 8, 128), BF16),
            pltpu.VMEM((16, 16, 128), BF16),
            pltpu.VMEM((16, 16, 128), BF16),
            dma((2,)),
            dma(()), dma(()),
            dma(()), dma((8,)),
            dma(()), dma(()),
            dma(()), dma(()),
            dma((8,)), dma((8,)),
            dma(()), dma(()),
            dma(()), dma(()),
        ],
        compiler_params=pltpu.CompilerParams(collective_id=0, has_side_effects=True),
    )(tasks, chol, amplitudes)


def local(chol, amplitudes, task_list, counts):
    tasks = compact(task_list, counts)
    got = ladder(tasks, chol, amplitudes)
    got = got.reshape(2, 2, 4, 2, 8, 2, 8, 8)
    return got.transpose(5, 3, 4, 2, 7, 0, 6, 1).reshape(4, 8, PAIRS)


def solution(mesh):
    placed = (P(None, "amp", "vec"), P(None, "amp", None), P(), P())
    return jax.shard_map(
        local, mesh=mesh, in_specs=placed, out_specs=P("vec", "amp", None), check_vma=False
    )
```

```python
import jax
import jax.numpy as jnp
from jax import lax
from jax.experimental import pallas as pl
from jax.experimental.pallas import tpu as pltpu
from jax.sharding import PartitionSpec as P

VB = 32
PAIRS = 1024
MOST = 2
TASKS = 32
N_AMP = 32
N_VEC = 16
MESH = pl.DeviceIdType.MESH
F32 = jnp.float32
BF16 = jnp.bfloat16
NT = (((1,), (1,)), ((), ()))


def compact_kernel(list_ref, counts_ref, out_ref):
    def one_list(w, position):
        for k in range(4):
            out_ref[position * 4 + k] = list_ref[k, w * MOST]
        position = position + jnp.minimum(counts_ref[w], 1)
        for k in range(4):
            out_ref[position * 4 + k] = list_ref[k, w * MOST + 1]
        return position + jnp.maximum(counts_ref[w] - 1, 0)

    lax.fori_loop(0, N_AMP, one_list, 0)


def compact(task_list, counts):
    return pl.pallas_call(
        compact_kernel,
        out_shape=jax.ShapeDtypeStruct(((TASKS + 1) * 4,), jnp.int32),
        in_specs=[pl.BlockSpec(memory_space=pltpu.SMEM)] * 2,
        out_specs=pl.BlockSpec(memory_space=pltpu.SMEM),
    )(task_list, counts)


def shift_of(q):
    return ((q + 1) // 2) * (2 * (q % 2) - 1)


def arrived(block, sem):
    pltpu.make_async_copy(block, block, sem).wait()


def ladder_kernel(
    task_ref, chol_hbm, amp_hbm, out_ref,
    chol_v, amp_v, xs, ys, ts, xr, yr, tr, xp, tfull, qs, order, vs, vr, ssum, keys, s2s, s2r, s3s, s3r,
    in_sem, x_send, x_recv, y_send, y_recv, t_send, t_recv, tv_send, tv_recv,
    v_send, v_recv, s2_send, s2_recv, s3_send, s3_recv,
):
    v = lax.axis_index("vec")
    m = lax.axis_index("amp")
    y, x_hi = v // 2, v % 2
    x_lo, z, core = m // 16, (m // 2) % 8, m % 2

    x_of = [x_lo * 16, (1 - x_lo) * 16]
    z_of = [(z + step) % 8 * 2 for step in (0, 7, 1, 6, 2, 5, 3, 4)]
    core_of = [core, 1 - core]
    y_of = [(y + step) % 8 * 2 for step in (0, 7, 1, 6, 2, 5, 3, 4)]
    hi_of = [x_hi, 1 - x_hi]

    def amp_peers(groups):
        for q in groups:
            for dx, dc in ((1, 1), (1, 0), (0, 1), (0, 0)):
                if q or dx or dc:
                    yield q, x_of[dx] + z_of[q] + core_of[dc]

    def vec_peers():
        for q in range(7, -1, -1):
            for dh in (1, 0):
                if q or dh:
                    yield y_of[q] + hi_of[dh]

    near, far = range(8), range(7, -1, -1)

    def to_amp(src, dst, send, recv, peer):
        pltpu.make_async_remote_copy(
            src_ref=src, dst_ref=dst, send_sem=send, recv_sem=recv,
            device_id={"amp": peer}, device_id_type=MESH,
        ).start()

    def to_vec(src, dst, send, recv, peer):
        pltpu.make_async_remote_copy(
            src_ref=src, dst_ref=dst, send_sem=send, recv_sem=recv,
            device_id={"vec": peer}, device_id_type=MESH,
        ).start()

    load_amp = pltpu.make_async_copy(amp_hbm, amp_v, in_sem.at[0])
    load_chol = pltpu.make_async_copy(chol_hbm, chol_v, in_sem.at[1])
    load_amp.start()
    load_chol.start()

    barrier = pltpu.get_barrier_semaphore()

    for _, peer in amp_peers(far):
        pl.semaphore_signal(barrier, inc=1, device_id={"amp": peer}, device_id_type=MESH)
    for peer in vec_peers():
        pl.semaphore_signal(barrier, inc=1, device_id={"vec": peer}, device_id_type=MESH)

    load_amp.wait()
    columns = pl.ds(pl.multiple_of(y * 128, 128), 128)

    @pl.loop(0, TASKS)
    def _(t):
        ts[t] = amp_v[task_ref[t * 4 + 2], :, columns]

    load_chol.wait()

    @pl.loop(0, TASKS)
    def _(t):
        xs[t] = chol_v[task_ref[t * 4]]
        ys[t] = chol_v[task_ref[t * 4 + 1]]

    pl.semaphore_wait(barrier, N_AMP + N_VEC - 2)

    @pl.when(core == x_hi)
    def _():
        pltpu.make_async_copy(ts.at[m], tr.at[v, m // 2], t_recv).start()

        for _, peer in amp_peers(far):
            to_amp(ts.at[peer], tr.at[v, m // 2], t_send, t_recv, peer)

    pltpu.make_async_copy(xs.at[m], xr.at[m], x_recv).start()

    for _, peer in amp_peers(near):
        to_amp(xs.at[peer], xr.at[m], x_send, x_recv, peer)

    pltpu.make_async_copy(ys.at[m], yr.at[x_lo, z, core], y_recv.at[0]).start()

    for q, peer in amp_peers(near):
        to_amp(ys.at[peer], yr.at[x_lo, z, core], y_send, y_recv.at[q], peer)

    arrived(tr.at[v], t_recv)

    for peer in vec_peers():
        to_vec(tr.at[v], tr.at[v], tv_send, tv_recv, peer)

    lane = lax.broadcasted_iota(jnp.int32, (8, 256), 1)

    def place(t, held):
        return jnp.where(lane // 8 == t, task_ref[t * 4 + 3] * 8 + lane % 8, held)

    wanted = lax.fori_loop(0, TASKS, place, jnp.zeros((8, 256), jnp.int32))[:1]

    @pl.loop(0, 4)
    def _(k):
        rows = lax.broadcasted_iota(jnp.int32, (128, 256), 0) + k * 128
        keys[pl.ds(pl.multiple_of(k * 128, 128), 128), :] = jnp.where(rows == wanted, 1.0, 0.0).astype(BF16)

    rows = lax.broadcasted_iota(jnp.int32, (128, 128), 0)
    cols = lax.broadcasted_iota(jnp.int32, (128, 128), 1)
    order[...] = jnp.where(cols == (rows % 4) * 32 + rows // 4, 1.0, 0.0).astype(BF16)

    arrived(xr, x_recv)

    @pl.loop(0, 8)
    def _(k):
        rows = lax.broadcasted_iota(jnp.int32, (128, 1024), 0) + k * 128
        cols = lax.broadcasted_iota(jnp.int32, (128, 1024), 1)
        pick = jnp.where(cols == (rows % 32) * 32 + rows // 32, 1.0, 0.0).astype(BF16)
        xp[pl.ds(pl.multiple_of(k * 128, 128), 128), :] = jnp.dot(
            pick, xr[...].reshape(PAIRS, 512), preferred_element_type=F32
        ).astype(BF16)

    arrived(tr.at[pl.ds(0, N_VEC - 1)], tv_recv)

    @pl.loop(0, 16)
    def _(k):
        for c in range(8):
            both = [
                jnp.concatenate([tr[2 * c, k].astype(F32), tr[2 * c + 1, k].astype(F32)], axis=0)
            ]
            tfull[pl.ds(pl.multiple_of(k * 16, 16), 16), c * 128 : c * 128 + 128] = both[0].astype(BF16)

    lanes = lax.broadcasted_iota(jnp.int32, (32, 128), 1)
    low_half = lanes < 64
    even = (lanes // 32) % 2 == 0

    @pl.loop(0, 8)
    def _(q):
        from_z = (z + shift_of(q) + 8) % 8
        arrived(yr.at[0, pl.ds(0, 2)], y_recv.at[q])
        y_rows = jnp.concatenate(
            [yr[0, from_z].reshape(64, 512), yr[1, from_z].reshape(64, 512)], axis=0
        )
        for k in range(8):
            block = lax.dot_general(
                xp[k * 128 : k * 128 + 128, :], y_rows, NT, preferred_element_type=F32
            )
            p0, p1, p2, p3 = (block[c * 32 : c * 32 + 32] for c in range(4))
            a0 = jnp.where(low_half, p0, pltpu.roll(p2, 64, 1))
            a2 = jnp.where(low_half, pltpu.roll(p0, 64, 1), p2)
            a1 = jnp.where(low_half, p1, pltpu.roll(p3, 64, 1))
            a3 = jnp.where(low_half, pltpu.roll(p1, 64, 1), p3)
            w = (
                jnp.where(even, a0, pltpu.roll(a1, 32, 1)),
                jnp.where(even, pltpu.roll(a0, 96, 1), a1),
                jnp.where(even, a2, pltpu.roll(a3, 32, 1)),
                jnp.where(even, pltpu.roll(a2, 96, 1), a3),
            )
            for b in range(4):
                qs[b * 32 : b * 32 + 32, k * 128 : k * 128 + 128] = w[b].astype(BF16)
        term = lax.dot_general(qs[...], tfull[...], NT, preferred_element_type=F32)
        term = jnp.dot(order[...], term.astype(BF16), preferred_element_type=F32)
        for k in range(N_VEC):
            vs[q, k] = term[k * 8 : k * 8 + 8].astype(BF16)

        pltpu.make_async_copy(vs.at[q, v], vr.at[q, v], v_recv.at[q]).start()

        for peer in vec_peers():
            to_vec(vs.at[q, peer], vr.at[q, v], v_send.at[q], v_recv.at[q], peer)

    @pl.loop(0, 8)
    def _(q):
        from_z = (z + shift_of(q) + 8) % 8
        arrived(vr.at[q], v_recv.at[q])
        total = vr[q, 0].astype(F32)
        for k in range(1, N_VEC):
            total += vr[q, k].astype(F32)
        high = total.astype(BF16).astype(F32)
        low = total - high
        for k in range(8):
            row = (k // 4) * 32 + ((k // 2) % 2) * 16 + from_z * 2 + k % 2
            ssum[pl.ds(row, 1), :] = high[k : k + 1]
            ssum[pl.ds(row + 64, 1), :] = low[k : k + 1]

    turned = ssum[...].T
    for k in range(N_AMP):
        s2s[k] = turned[k * 8 : k * 8 + 8].astype(BF16)

    pltpu.make_async_copy(s2s.at[m], s2r.at[m], s2_recv).start()

    for _, peer in amp_peers(far):
        to_amp(s2s.at[peer], s2r.at[m], s2_send, s2_recv, peer)

    arrived(s2r, s2_recv)
    parts = s2r[...].astype(F32).reshape(256, 128).astype(BF16)
    tiles = jnp.dot(keys[...], parts, preferred_element_type=F32)
    tiles = tiles + pltpu.roll(tiles, 64, 1)
    low16 = lax.broadcasted_iota(jnp.int32, (16, 128), 1) < 64
    for k in range(N_VEC):
        s3s[k] = jnp.where(
            low16, tiles[k * 32 : k * 32 + 16], tiles[k * 32 + 16 : k * 32 + 32]
        ).astype(BF16)

    pltpu.make_async_copy(s3s.at[v], s3r.at[v], s3_recv).start()

    for peer in vec_peers():
        to_vec(s3s.at[peer], s3r.at[v], s3_send, s3_recv, peer)

    arrived(s3r, s3_recv)
    for k in range(0, N_VEC, 2):
        left, right = s3r[k].astype(F32), s3r[k + 1].astype(F32)
        upper = jnp.where(low16, left, pltpu.roll(right, 64, 1)).astype(BF16)
        lower = jnp.where(low16, pltpu.roll(left, 64, 1), right).astype(BF16)
        for p, rows in enumerate((upper[:8], upper[8:], lower[:8], lower[8:])):
            out_ref[p, :, k * 64 : k * 64 + 128] = rows

    @pl.when(core == x_hi)
    def _():
        arrived(ts.at[pl.ds(0, N_AMP - 1)], t_send)

    arrived(xs.at[pl.ds(0, N_AMP - 1)], x_send)
    arrived(ys.at[pl.ds(0, N_AMP - 1)], y_send)
    arrived(tr.at[pl.ds(0, N_VEC - 1)], tv_send)

    @pl.loop(0, 8)
    def _(q):
        arrived(vs.at[q, pl.ds(0, N_VEC - 1)], v_send.at[q])

    arrived(s2s.at[pl.ds(0, N_AMP - 1)], s2_send)
    arrived(s3s.at[pl.ds(0, N_VEC - 1)], s3_send)


def ladder(tasks, chol, amplitudes):
    dma = pltpu.SemaphoreType.DMA
    return pl.pallas_call(
        ladder_kernel,
        out_shape=jax.ShapeDtypeStruct((4, 8, PAIRS), BF16),
        in_specs=[
            pl.BlockSpec(memory_space=pltpu.SMEM),
            pl.BlockSpec(memory_space=pl.ANY),
            pl.BlockSpec(memory_space=pl.ANY),
        ],
        out_specs=pl.BlockSpec(memory_space=pltpu.VMEM),
        scratch_shapes=[
            pltpu.VMEM((64, 32, 512), BF16),
            pltpu.VMEM((64, 8, 1024), BF16),
            pltpu.VMEM((32, 32, 512), BF16),
            pltpu.VMEM((32, 32, 512), BF16),
            pltpu.VMEM((32, 8, 128), BF16),
            pltpu.VMEM((32, 32, 512), BF16),
            pltpu.VMEM((2, 8, 2, 32, 512), BF16),
            pltpu.VMEM((16, 16, 8, 128), BF16),
            pltpu.VMEM((1024, 512), BF16),
            pltpu.VMEM((256, 1024), BF16),
            pltpu.VMEM((128, 1024), BF16),
            pltpu.VMEM((128, 128), BF16),
            pltpu.VMEM((8, 16, 8, 256), BF16),
            pltpu.VMEM((8, 16, 8, 256), BF16),
            pltpu.VMEM((128, 256), F32),
            pltpu.VMEM((512, 256), BF16),
            pltpu.VMEM((32, 8, 128), BF16),
            pltpu.VMEM((32, 8, 128), BF16),
            pltpu.VMEM((16, 16, 128), BF16),
            pltpu.VMEM((16, 16, 128), BF16),
            dma((2,)),
            dma(()), dma(()),
            dma(()), dma((8,)),
            dma(()), dma(()),
            dma(()), dma(()),
            dma((8,)), dma((8,)),
            dma(()), dma(()),
            dma(()), dma(()),
        ],
        compiler_params=pltpu.CompilerParams(collective_id=0, has_side_effects=True),
    )(tasks, chol, amplitudes)


def local(chol, amplitudes, task_list, counts):
    return ladder(compact(task_list.T, counts), chol, amplitudes)


def solution(mesh):
    placed = (P(None, "amp", "vec"), P(None, "amp", None), P(), P())
    return jax.shard_map(
        local, mesh=mesh, in_specs=placed, out_specs=P("vec", "amp", None), check_vma=False
    )
```

```python
import jax
import jax.numpy as jnp
from jax import lax
from jax.experimental import pallas as pl
from jax.experimental.pallas import tpu as pltpu
from jax.sharding import PartitionSpec as P

VB = 32
PAIRS = 1024
MOST = 2
TASKS = 32
N_AMP = 32
N_VEC = 16
MESH = pl.DeviceIdType.MESH
F32 = jnp.float32
BF16 = jnp.bfloat16
NT = (((1,), (1,)), ((), ()))


def compact_kernel(list_ref, counts_ref, out_ref):
    def one_list(w, position):
        for k in range(4):
            out_ref[position * 4 + k] = list_ref[k, w * MOST]
        position = position + jnp.minimum(counts_ref[w], 1)
        for k in range(4):
            out_ref[position * 4 + k] = list_ref[k, w * MOST + 1]
        return position + jnp.maximum(counts_ref[w] - 1, 0)

    lax.fori_loop(0, N_AMP, one_list, 0)


def compact(task_list, counts):
    return pl.pallas_call(
        compact_kernel,
        out_shape=jax.ShapeDtypeStruct(((TASKS + 1) * 4,), jnp.int32),
        in_specs=[pl.BlockSpec(memory_space=pltpu.SMEM)] * 2,
        out_specs=pl.BlockSpec(memory_space=pltpu.SMEM),
    )(task_list, counts)


def shift_of(q):
    return ((q + 1) // 2) * (2 * (q % 2) - 1)


def arrived(block, sem):
    pltpu.make_async_copy(block, block, sem).wait()


def ladder_kernel(
    task_ref, chol_hbm, amp_hbm, out_ref,
    out_v, chol_v, amp_v, xs, ys, ts, xr, yr, tr, xp, tfull, qs, order, vs, vr, ssum, keys, s2s, s2r, s3s, s3r,
    in_sem, x_send, x_recv, y_send, y_recv, t_send, t_recv, tv_send, tv_recv,
    v_send, v_recv, s2_send, s2_recv, s3_send, s3_recv,
):
    v = lax.axis_index("vec")
    m = lax.axis_index("amp")
    y, x_hi = v // 2, v % 2
    x_lo, z, core = m // 16, (m // 2) % 8, m % 2

    x_of = [x_lo * 16, (1 - x_lo) * 16]
    z_of = [(z + step) % 8 * 2 for step in (0, 7, 1, 6, 2, 5, 3, 4)]
    core_of = [core, 1 - core]
    y_of = [(y + step) % 8 * 2 for step in (0, 7, 1, 6, 2, 5, 3, 4)]
    hi_of = [x_hi, 1 - x_hi]

    def amp_peers(groups):
        for q in groups:
            for dx, dc in ((1, 1), (1, 0), (0, 1), (0, 0)):
                if q or dx or dc:
                    yield q, x_of[dx] + z_of[q] + core_of[dc]

    def vec_peers():
        for q in range(7, -1, -1):
            for dh in (1, 0):
                if q or dh:
                    yield y_of[q] + hi_of[dh]

    near, far = range(8), range(7, -1, -1)

    def to_amp(src, dst, send, recv, peer):
        pltpu.make_async_remote_copy(
            src_ref=src, dst_ref=dst, send_sem=send, recv_sem=recv,
            device_id={"amp": peer}, device_id_type=MESH,
        ).start()

    def to_vec(src, dst, send, recv, peer):
        pltpu.make_async_remote_copy(
            src_ref=src, dst_ref=dst, send_sem=send, recv_sem=recv,
            device_id={"vec": peer}, device_id_type=MESH,
        ).start()

    load_amp = pltpu.make_async_copy(amp_hbm, amp_v, in_sem.at[0])
    load_chol = pltpu.make_async_copy(chol_hbm, chol_v, in_sem.at[1])
    load_amp.start()
    load_chol.start()

    barrier = pltpu.get_barrier_semaphore()

    for _, peer in amp_peers(far):
        pl.semaphore_signal(barrier, inc=1, device_id={"amp": peer}, device_id_type=MESH)
    for peer in vec_peers():
        pl.semaphore_signal(barrier, inc=1, device_id={"vec": peer}, device_id_type=MESH)

    load_amp.wait()
    columns = pl.ds(pl.multiple_of(y * 128, 128), 128)

    @pl.loop(0, TASKS)
    def _(t):
        ts[t] = amp_v[task_ref[t * 4 + 2], :, columns]

    load_chol.wait()

    @pl.loop(0, TASKS)
    def _(t):
        xs[t] = chol_v[task_ref[t * 4]]
        ys[t] = chol_v[task_ref[t * 4 + 1]]

    pl.semaphore_wait(barrier, N_AMP + N_VEC - 2)

    @pl.when(core == x_hi)
    def _():
        pltpu.make_async_copy(ts.at[m], tr.at[v, m // 2], t_recv).start()

        for _, peer in amp_peers(far):
            to_amp(ts.at[peer], tr.at[v, m // 2], t_send, t_recv, peer)

    pltpu.make_async_copy(xs.at[m], xr.at[m], x_recv).start()

    for _, peer in amp_peers(near):
        to_amp(xs.at[peer], xr.at[m], x_send, x_recv, peer)

    pltpu.make_async_copy(ys.at[m], yr.at[x_lo, z, core], y_recv.at[0]).start()

    for q, peer in amp_peers(near):
        to_amp(ys.at[peer], yr.at[x_lo, z, core], y_send, y_recv.at[q], peer)

    arrived(tr.at[v], t_recv)

    for peer in vec_peers():
        to_vec(tr.at[v], tr.at[v], tv_send, tv_recv, peer)

    lane = lax.broadcasted_iota(jnp.int32, (8, 256), 1)

    def place(t, held):
        return jnp.where(lane // 8 == t, task_ref[t * 4 + 3] * 8 + lane % 8, held)

    wanted = lax.fori_loop(0, TASKS, place, jnp.zeros((8, 256), jnp.int32))[:1]

    @pl.loop(0, 4)
    def _(k):
        rows = lax.broadcasted_iota(jnp.int32, (128, 256), 0) + k * 128
        keys[pl.ds(pl.multiple_of(k * 128, 128), 128), :] = jnp.where(rows == wanted, 1.0, 0.0).astype(BF16)

    rows = lax.broadcasted_iota(jnp.int32, (128, 128), 0)
    cols = lax.broadcasted_iota(jnp.int32, (128, 128), 1)
    order[...] = jnp.where(cols == (rows % 4) * 32 + rows // 4, 1.0, 0.0).astype(BF16)

    arrived(xr, x_recv)

    @pl.loop(0, 8)
    def _(k):
        rows = lax.broadcasted_iota(jnp.int32, (128, 1024), 0) + k * 128
        cols = lax.broadcasted_iota(jnp.int32, (128, 1024), 1)
        pick = jnp.where(cols == (rows % 32) * 32 + rows // 32, 1.0, 0.0).astype(BF16)
        xp[pl.ds(pl.multiple_of(k * 128, 128), 128), :] = jnp.dot(
            pick, xr[...].reshape(PAIRS, 512), preferred_element_type=F32
        ).astype(BF16)

    arrived(tr.at[pl.ds(0, N_VEC - 1)], tv_recv)

    @pl.loop(0, 16)
    def _(k):
        for c in range(8):
            both = [
                jnp.concatenate([tr[2 * c, k].astype(F32), tr[2 * c + 1, k].astype(F32)], axis=0)
            ]
            tfull[pl.ds(pl.multiple_of(k * 16, 16), 16), c * 128 : c * 128 + 128] = both[0].astype(BF16)

    lanes = lax.broadcasted_iota(jnp.int32, (32, 128), 1)
    low_half = lanes < 64
    even = (lanes // 32) % 2 == 0

    @pl.loop(0, 8)
    def _(q):
        from_z = (z + shift_of(q) + 8) % 8
        arrived(yr.at[0, pl.ds(0, 2)], y_recv.at[q])
        y_rows = jnp.concatenate(
            [yr[0, from_z].reshape(64, 512), yr[1, from_z].reshape(64, 512)], axis=0
        )
        for k in range(8):
            block = lax.dot_general(
                xp[k * 128 : k * 128 + 128, :], y_rows, NT, preferred_element_type=F32
            )
            p0, p1, p2, p3 = (block[c * 32 : c * 32 + 32] for c in range(4))
            a0 = jnp.where(low_half, p0, pltpu.roll(p2, 64, 1))
            a2 = jnp.where(low_half, pltpu.roll(p0, 64, 1), p2)
            a1 = jnp.where(low_half, p1, pltpu.roll(p3, 64, 1))
            a3 = jnp.where(low_half, pltpu.roll(p1, 64, 1), p3)
            w = (
                jnp.where(even, a0, pltpu.roll(a1, 32, 1)),
                jnp.where(even, pltpu.roll(a0, 96, 1), a1),
                jnp.where(even, a2, pltpu.roll(a3, 32, 1)),
                jnp.where(even, pltpu.roll(a2, 96, 1), a3),
            )
            for b in range(4):
                qs[b * 32 : b * 32 + 32, k * 128 : k * 128 + 128] = w[b].astype(BF16)
        term = lax.dot_general(qs[...], tfull[...], NT, preferred_element_type=F32)
        term = jnp.dot(order[...], term.astype(BF16), preferred_element_type=F32)
        for k in range(N_VEC):
            vs[q, k] = term[k * 8 : k * 8 + 8].astype(BF16)

        pltpu.make_async_copy(vs.at[q, v], vr.at[q, v], v_recv.at[q]).start()

        for peer in vec_peers():
            to_vec(vs.at[q, peer], vr.at[q, v], v_send.at[q], v_recv.at[q], peer)

    @pl.loop(0, 8)
    def _(q):
        from_z = (z + shift_of(q) + 8) % 8
        arrived(vr.at[q], v_recv.at[q])
        total = vr[q, 0].astype(F32)
        for k in range(1, N_VEC):
            total += vr[q, k].astype(F32)
        high = total.astype(BF16).astype(F32)
        low = total - high
        for k in range(8):
            row = (k // 4) * 32 + ((k // 2) % 2) * 16 + from_z * 2 + k % 2
            ssum[pl.ds(row, 1), :] = high[k : k + 1]
            ssum[pl.ds(row + 64, 1), :] = low[k : k + 1]

    turned = ssum[...].T
    for k in range(N_AMP):
        s2s[k] = turned[k * 8 : k * 8 + 8].astype(BF16)

    pltpu.make_async_copy(s2s.at[m], s2r.at[m], s2_recv).start()

    for _, peer in amp_peers(far):
        to_amp(s2s.at[peer], s2r.at[m], s2_send, s2_recv, peer)

    arrived(s2r, s2_recv)
    parts = s2r[...].astype(F32).reshape(256, 128).astype(BF16)
    tiles = jnp.dot(keys[...], parts, preferred_element_type=F32)
    tiles = tiles + pltpu.roll(tiles, 64, 1)
    low16 = lax.broadcasted_iota(jnp.int32, (16, 128), 1) < 64
    for k in range(N_VEC):
        s3s[k] = jnp.where(
            low16, tiles[k * 32 : k * 32 + 16], tiles[k * 32 + 16 : k * 32 + 32]
        ).astype(BF16)

    pltpu.make_async_copy(s3s.at[v], s3r.at[v], s3_recv).start()

    for peer in vec_peers():
        to_vec(s3s.at[peer], s3r.at[v], s3_send, s3_recv, peer)

    arrived(s3r, s3_recv)
    for k in range(0, N_VEC, 2):
        left, right = s3r[k].astype(F32), s3r[k + 1].astype(F32)
        upper = jnp.where(low16, left, pltpu.roll(right, 64, 1)).astype(BF16)
        lower = jnp.where(low16, pltpu.roll(left, 64, 1), right).astype(BF16)
        for p, rows in enumerate((upper[:8], upper[8:], lower[:8], lower[8:])):
            out_v[p, :, k * 64 : k * 64 + 128] = rows
    store = pltpu.make_async_copy(out_v, out_ref, in_sem.at[0])
    store.start()

    @pl.when(core == x_hi)
    def _():
        arrived(ts.at[pl.ds(0, N_AMP - 1)], t_send)

    arrived(xs.at[pl.ds(0, N_AMP - 1)], x_send)
    arrived(ys.at[pl.ds(0, N_AMP - 1)], y_send)
    arrived(tr.at[pl.ds(0, N_VEC - 1)], tv_send)

    @pl.loop(0, 8)
    def _(q):
        arrived(vs.at[q, pl.ds(0, N_VEC - 1)], v_send.at[q])

    arrived(s2s.at[pl.ds(0, N_AMP - 1)], s2_send)
    arrived(s3s.at[pl.ds(0, N_VEC - 1)], s3_send)
    store.wait()


def ladder(tasks, chol, amplitudes):
    dma = pltpu.SemaphoreType.DMA
    return pl.pallas_call(
        ladder_kernel,
        out_shape=jax.ShapeDtypeStruct((4, 8, PAIRS), BF16),
        in_specs=[
            pl.BlockSpec(memory_space=pltpu.SMEM),
            pl.BlockSpec(memory_space=pl.ANY),
            pl.BlockSpec(memory_space=pl.ANY),
        ],
        out_specs=pl.BlockSpec(memory_space=pl.ANY),
        scratch_shapes=[
            pltpu.VMEM((4, 8, PAIRS), BF16),
            pltpu.VMEM((64, 32, 512), BF16),
            pltpu.VMEM((64, 8, 1024), BF16),
            pltpu.VMEM((32, 32, 512), BF16),
            pltpu.VMEM((32, 32, 512), BF16),
            pltpu.VMEM((32, 8, 128), BF16),
            pltpu.VMEM((32, 32, 512), BF16),
            pltpu.VMEM((2, 8, 2, 32, 512), BF16),
            pltpu.VMEM((16, 16, 8, 128), BF16),
            pltpu.VMEM((1024, 512), BF16),
            pltpu.VMEM((256, 1024), BF16),
            pltpu.VMEM((128, 1024), BF16),
            pltpu.VMEM((128, 128), BF16),
            pltpu.VMEM((8, 16, 8, 256), BF16),
            pltpu.VMEM((8, 16, 8, 256), BF16),
            pltpu.VMEM((128, 256), F32),
            pltpu.VMEM((512, 256), BF16),
            pltpu.VMEM((32, 8, 128), BF16),
            pltpu.VMEM((32, 8, 128), BF16),
            pltpu.VMEM((16, 16, 128), BF16),
            pltpu.VMEM((16, 16, 128), BF16),
            dma((2,)),
            dma(()), dma(()),
            dma(()), dma((8,)),
            dma(()), dma(()),
            dma(()), dma(()),
            dma((8,)), dma((8,)),
            dma(()), dma(()),
            dma(()), dma(()),
        ],
        compiler_params=pltpu.CompilerParams(collective_id=0, has_side_effects=True, vmem_limit_bytes=55000 * 2**10),
    )(tasks, chol, amplitudes)


def local(chol, amplitudes, task_list, counts):
    return ladder(compact(task_list.T, counts), chol, amplitudes)


def solution(mesh):
    placed = (P(None, "amp", "vec"), P(None, "amp", None), P(), P())
    return jax.shard_map(
        local, mesh=mesh, in_specs=placed, out_specs=P("vec", "amp", None), check_vma=False
    )
```
